32 devices in a mesh: ctx: 8 (over z, x), head: 4 (over y, core).
Axes of the slice: x: 2, y: 2, z: 4, core: 2. Of those that a mesh axis runs over, the one named last changes fastest.
Arguments:
- attn_query: bfloat16 [4096, 6144], P('ctx', 'head'), may hold values from -16 to 16
- attn_key: bfloat16 [4096, 6144], P('ctx', 'head'), may hold values from -16 to 16
- attn_value: bfloat16 [4096, 6144], P('ctx', 'head'), may hold values from -120 to 120
- delta_query: bfloat16 [4096, 6144], P('ctx', 'head'), may hold values from -6 to 6
- delta_key: bfloat16 [4096, 6144], P('ctx', 'head'), may hold values from -6 to 6
- delta_value: bfloat16 [4096, 6144], P('ctx', 'head'), may hold values from -120 to 120
- delta_gate: float32 [4096, 48], P('ctx', 'head'), may hold values from 0.5 to 1
- delta_beta: float32 [4096, 48], P('ctx', 'head'), may hold values from 0 to 0.6, as said below
- attn_gain: float32 [6144], P('head'), may hold values from 0.1 to 1.9
- delta_gain: float32 [6144], P('head'), may hold values from 0.1 to 1.9
Outputs:
- mixed: bfloat16 [4096, 6144], P('ctx', 'head')
The draws below stay inside these ranges and needn't reach their ends.
Inputs may be any that keep to these rules, and one draw needn't show every extreme that they name: `delta_beta`: Positive.
All inputs are finite; a program needn't handle non-finite values.
Results may differ from the reference program's by a relative error of at most 0.004.
Values may be sent and summed in bfloat16 or wider, within the bound.
A program may use at most 192 MiB of HBM per device.

```python
import math
import jax
import jax.numpy as jnp
from jax import lax

HEAD_COUNT = 48
DH = 128
WIDTH = 6144
WINDOW = 1024
GROUP = 64
TOK_DEV = 512
TOKEN_COUNT = 4096


def drawn_pair(key):
    sequence_lanes = jax.random.split(jax.random.fold_in(key, 101), 2)
    queries = jnp.clip(jax.random.normal(sequence_lanes[0], (TOKEN_COUNT, HEAD_COUNT, DH), jnp.float32), -5.0, 5.0)
    keyvecs = jnp.clip(jax.random.normal(sequence_lanes[1], (TOKEN_COUNT, HEAD_COUNT, DH), jnp.float32), -5.0, 5.0)
    return (queries.reshape(TOKEN_COUNT, HEAD_COUNT * DH), keyvecs.reshape(TOKEN_COUNT, HEAD_COUNT * DH))


def scaled_values(key, salt):
    sequence_lanes = jax.random.split(jax.random.fold_in(key, salt), 1)
    values = jnp.clip(jax.random.normal(sequence_lanes[0], (TOKEN_COUNT, HEAD_COUNT, DH), jnp.float32), -4.0, 4.0)
    head_ramp = jnp.exp(math.log(3.0) * jnp.arange(HEAD_COUNT, dtype=jnp.float32) / max(HEAD_COUNT - 1, 1))
    values = values * head_ramp[None, :, None]
    return values.reshape(TOKEN_COUNT, HEAD_COUNT * DH)


def fast_heads(key):
    fraction = 0.5
    return jax.random.bernoulli(jax.random.fold_in(key, 202), fraction, (HEAD_COUNT,))


def draw_attn_query(key, part):
    return drawn_pair(key)[0].astype(jnp.bfloat16)


def draw_attn_key(key, part):
    return drawn_pair(key)[1].astype(jnp.bfloat16)


def draw_attn_value(key, part):
    return scaled_values(key, 303).astype(jnp.bfloat16)


def draw_delta_value(key, part):
    return scaled_values(key, 404).astype(jnp.bfloat16)


def draw_delta_key(key, part):
    rapid_heads = fast_heads(key)
    sequence_lanes = jax.random.split(jax.random.fold_in(key, 707), 3)
    sub_dims = max(DH * 3 // 16, 2)
    shard_count = TOKEN_COUNT // TOK_DEV
    background = jax.random.normal(sequence_lanes[0], (shard_count, TOK_DEV, HEAD_COUNT, DH), jnp.float32)
    directions = jax.random.normal(sequence_lanes[1], (shard_count, HEAD_COUNT, sub_dims, DH), jnp.float32) / math.sqrt(DH)
    loadings = jax.random.normal(sequence_lanes[2], (shard_count, TOK_DEV, HEAD_COUNT, sub_dims), jnp.float32)
    focused = 4.0 * jnp.einsum('bths,bhsd->bthd', loadings, directions)
    keyvecs = background + jnp.where(rapid_heads[None, None, :, None], 0.0, focused)
    keyvecs = jnp.clip(keyvecs, -6.0, 6.0)
    return keyvecs.reshape(TOKEN_COUNT, HEAD_COUNT * DH).astype(jnp.bfloat16)


def draw_delta_gate(key, part):
    rapid_heads = fast_heads(key)
    sequence_lanes = jax.random.split(jax.random.fold_in(key, 505), 3)
    roughness = jnp.exp(jax.random.uniform(sequence_lanes[0], (TOKEN_COUNT, HEAD_COUNT), jnp.float32, math.log(0.5), math.log(2.0)))
    log_decay_rates = jnp.where(rapid_heads[None, :], 1.0 / 40.0, 0.5 / TOKEN_COUNT) * roughness
    token_groups = jax.random.bernoulli(sequence_lanes[1], 2.0 / TOKEN_COUNT, (TOKEN_COUNT, HEAD_COUNT)) & jnp.logical_not(rapid_heads)[None, :]
    removed_entries = jax.random.uniform(sequence_lanes[2], (TOKEN_COUNT, HEAD_COUNT), jnp.float32, 0.5, 0.8)
    return jnp.where(token_groups, removed_entries, jnp.exp(-log_decay_rates)).astype(jnp.float32)


def draw_delta_beta(key, part):
    rapid_heads = fast_heads(key)
    roughness = jnp.exp(jax.random.uniform(jax.random.fold_in(key, 606), (TOKEN_COUNT, HEAD_COUNT), jnp.float32, math.log(0.5), math.log(2.0)))
    baseline = jnp.where(rapid_heads[None, :], 0.25, float(DH) / TOKEN_COUNT)
    return jnp.minimum(baseline * roughness, 0.6).astype(jnp.float32)


def steps_of(own_key, extent, cuts, low, high):
    gain = 1.0
    for dim, shards_of in cuts:
        steps = jax.random.uniform(jax.random.fold_in(jax.random.fold_in(own_key, 6), dim), (shards_of,), jnp.float32, low / len(cuts), high / len(cuts))
        gain = gain * jnp.repeat(jnp.exp(steps), extent[dim] // shards_of).reshape((-1,) + (1,) * (len(extent) - 1 - dim))
    return gain


def normal_values(rng, shape, scale, limit, cuts=(), held_as=jnp.bfloat16):
    gain = steps_of(rng, shape, cuts, -0.22, 0.18) if cuts else 1.0
    values = jax.random.normal(rng, shape, jnp.float32) * scale * gain
    return jnp.minimum(jnp.maximum(values, -limit), limit).astype(held_as)


def setup_inputs(seed: int = 0) -> dict:
    keys = jax.random.split(jax.random.key(seed), 11)
    return {
        "attn_query": draw_attn_query(jax.random.fold_in(keys[10], 71), 0),
        "attn_key": draw_attn_key(jax.random.fold_in(keys[10], 71), 0),
        "attn_value": draw_attn_value(jax.random.fold_in(keys[10], 71), 0),
        "delta_query": normal_values(keys[3], (TOKEN_COUNT, WIDTH), 1.0, 6.0, ((0, 8), (1, 4))),
        "delta_key": draw_delta_key(jax.random.fold_in(keys[10], 71), 0),
        "delta_value": draw_delta_value(jax.random.fold_in(keys[10], 71), 0),
        "delta_gate": draw_delta_gate(jax.random.fold_in(keys[10], 71), 0),
        "delta_beta": draw_delta_beta(jax.random.fold_in(keys[10], 71), 0),
        "attn_gain": jnp.clip(1.0 + 0.18 * jax.random.normal(keys[8], (WIDTH,), jnp.float32), 0.1, 1.9),
        "delta_gain": jnp.clip(1.0 + 0.18 * jax.random.normal(keys[9], (WIDTH,), jnp.float32), 0.1, 1.9),
    }


epsilon = 1e-06
highest = lax.Precision.HIGHEST

def unit_rows(values):
    return values * lax.rsqrt(lax.optimization_barrier(jnp.mean(values * values, axis=-1, keepdims=True)) + epsilon) / math.sqrt(values.shape[-1])

def group_terms(inputs):
    queries, keyvecs, values, alphas, betas = inputs
    length = alphas.shape[0]
    log_sums = jnp.cumsum(jnp.log(alphas), axis=0)
    causal = jnp.arange(length, dtype=jnp.int32)[:, None] >= jnp.arange(length, dtype=jnp.int32)[None, :]
    spread = log_sums.T[:, :, None] - log_sums.T[:, None, :]
    ratios = jnp.exp(jnp.where(causal[None], spread, -1e+30))
    identity = jnp.eye(length, dtype=jnp.float32)
    key_gram = jnp.einsum('rhd,shd->hrs', keyvecs, keyvecs, precision=highest)
    negated = -(betas.T[:, :, None] * ratios * (1.0 - identity) * key_gram)
    inverse = identity + negated
    powered = negated
    for doubling in range(max((length - 1).bit_length() - 1, 0)):
        powered = jnp.einsum('hij,hjk->hik', powered, powered, precision=highest)
        inverse = inverse + jnp.einsum('hij,hjk->hik', inverse, powered, precision=highest)
    growth = jnp.exp(log_sums)
    scaled_vals = jnp.transpose(betas[:, :, None] * values, (1, 0, 2))
    scaled_keys = jnp.transpose((betas * growth)[:, :, None] * keyvecs, (1, 0, 2))
    pseudo_vals = jnp.einsum('hij,hjd->hid', inverse, scaled_vals, precision=highest)
    pseudo_keys = jnp.einsum('hij,hjd->hid', inverse, scaled_keys, precision=highest)
    decay_tail = jnp.exp(log_sums[-1][:, None] - log_sums.T)
    return (log_sums, ratios, growth, decay_tail, pseudo_vals, pseudo_keys)

def group_step(current, inputs):
    queries, keyvecs, values, alphas, betas = inputs
    log_sums, ratios, growth, decay_tail, pseudo_vals, pseudo_keys = group_terms(inputs)
    errors = pseudo_vals - jnp.einsum('hcd,hde->hce', pseudo_keys, current, precision=highest)
    mixing = jnp.einsum('rhd,shd->hrs', queries, keyvecs, precision=highest) * ratios
    outputs = growth.T[:, :, None] * jnp.einsum('chd,hde->hce', queries, current, precision=highest)
    outputs = outputs + jnp.einsum('hrs,hse->hre', mixing, errors, precision=highest)
    new_state = jnp.exp(log_sums[-1])[:, None, None] * current
    new_state = new_state + jnp.einsum('chd,hc,hce->hde', keyvecs, decay_tail, errors, precision=highest)
    return (new_state, jnp.transpose(outputs, (1, 0, 2)))

def delta_inputs(queries, keyvecs, values, alphas, betas):
    length = alphas.shape[0]
    count = alphas.shape[1]
    blocks = length // GROUP

    def to_blocks(array):
        return array.astype(jnp.float32).reshape(blocks, GROUP, count, DH)
    return (unit_rows(to_blocks(queries)), unit_rows(to_blocks(keyvecs)), to_blocks(values), alphas.reshape(blocks, GROUP, count), betas.reshape(blocks, GROUP, count))

def attend(queries, keyvecs, values, query_start, key_start):
    scores = jnp.einsum('qhd,khd->hqk', queries.astype(jnp.float32), keyvecs.astype(jnp.float32)) / math.sqrt(queries.shape[-1])
    query_pos = query_start + jnp.arange(queries.shape[0], dtype=jnp.int32)[:, None]
    key_pos = key_start + jnp.arange(keyvecs.shape[0], dtype=jnp.int32)[None, :]
    distance = query_pos - key_pos
    allowed = (distance >= 0) & (distance < WINDOW) & (key_pos >= 0)
    scores = jnp.where(allowed[None], scores, -1e+30)
    maxima = lax.optimization_barrier(jnp.max(scores, axis=-1, keepdims=True))
    raised = jnp.exp(scores - maxima)
    weights = (raised / lax.optimization_barrier(jnp.sum(raised, axis=-1, keepdims=True))).astype(jnp.bfloat16)
    return jnp.einsum('hqk,khd->qhd', weights.astype(jnp.float32), values.astype(jnp.float32))

def window_attention(queries, keyvecs, values):
    length = queries.shape[0]
    block_rows = math.gcd(length, 512)
    padded_keys = jnp.concatenate([jnp.zeros((WINDOW, WIDTH), jnp.bfloat16), keyvecs], axis=0)
    padded_vals = jnp.concatenate([jnp.zeros((WINDOW, WIDTH), jnp.bfloat16), values], axis=0)

    def one_block(start):
        query_blk = lax.dynamic_slice_in_dim(queries, start, block_rows, 0).reshape(block_rows, HEAD_COUNT, DH)
        key_blk = lax.dynamic_slice_in_dim(padded_keys, start, block_rows + WINDOW, 0).reshape(block_rows + WINDOW, HEAD_COUNT, DH)
        value_blk = lax.dynamic_slice_in_dim(padded_vals, start, block_rows + WINDOW, 0).reshape(block_rows + WINDOW, HEAD_COUNT, DH)
        return attend(query_blk, key_blk, value_blk, start, start - WINDOW)
    starts = jnp.arange(length // block_rows, dtype=jnp.int32) * block_rows
    outputs = lax.map(one_block, starts)
    return outputs.reshape(length, WIDTH)

def reference(attn_query, attn_key, attn_value, delta_query, delta_key, delta_value, delta_gate, delta_beta, attn_gain, delta_gain):
    attn_out = window_attention(attn_query, attn_key, attn_value)
    prepared = delta_inputs(delta_query, delta_key, delta_value, delta_gate, delta_beta)
    current = jnp.zeros((HEAD_COUNT, DH, DH), jnp.float32)
    final_state, delta_blocks = lax.scan(group_step, current, prepared)
    delta_out = delta_blocks.reshape(TOKEN_COUNT, WIDTH)
    scale_attn = lax.rsqrt(lax.optimization_barrier(jnp.mean(attn_out * attn_out, axis=-1, keepdims=True)) + epsilon)
    scale_delta = lax.rsqrt(lax.optimization_barrier(jnp.mean(delta_out * delta_out, axis=-1, keepdims=True)) + epsilon)
    joined = 0.5 * (attn_gain * attn_out * scale_attn + delta_gain * delta_out * scale_delta)
    return joined.astype(jnp.bfloat16)
```

```python
import functools
import math

import jax
import jax.numpy as jnp
from jax import lax
from jax.experimental import pallas as pl
from jax.experimental.pallas import tpu as pltpu
from jax.sharding import PartitionSpec as P

DH = 128
WINDOW = 1024
CHUNK = 128
QROWS = 256
HEADS_STEP = 2

epsilon = 1e-06
f32 = jnp.float32
bf16 = jnp.bfloat16


def dot(left, right, dims=((1,), (0,))):
    return lax.dot_general(left, right, (dims, ((), ())), preferred_element_type=f32)


def dot1(left, right, dims=((1,), (0,))):
    return dot(left.astype(bf16), right.astype(bf16), dims)


def split(value):
    high = value.astype(bf16)
    return high, (value - high.astype(f32)).astype(bf16)


def dot3(left, right, dims=((1,), (0,))):
    lh, ll = split(left)
    rh, rl = split(right)
    return dot(lh, rh, dims) + (dot(lh, rl, dims) + dot(ll, rh, dims))


def unit_scale(raw):
    wide = raw.astype(f32)
    mean = jnp.mean(wide * wide, axis=-1, keepdims=True)
    return lax.rsqrt(mean + epsilon) / math.sqrt(DH)


def delta_kernel(q_ref, k_ref, v_ref, gate_ref, beta_ref, out_ref, qeff_ref, lin_ref, off_ref):
    rows = q_ref.shape[0]
    chunks = rows // CHUNK
    ri = lax.broadcasted_iota(jnp.int32, (CHUNK, CHUNK), 0)
    ci = lax.broadcasted_iota(jnp.int32, (CHUNK, CHUNK), 1)
    eye = ri == ci
    lower = ri >= ci
    strict = ri > ci
    identity = jnp.where(eye, 1.0, 0.0).astype(f32)

    def column(row):
        return jnp.sum(jnp.where(eye, row, 0.0), axis=1, keepdims=True)

    def as_row(col):
        return jnp.sum(jnp.where(eye, col, 0.0), axis=0, keepdims=True)

    units = [(h, c) for c in range(chunks) for h in range(HEADS_STEP)]
    terms = {}
    for h, c in units:
        rs = slice(c * CHUNK, (c + 1) * CHUNK)
        cs = slice(h * DH, (h + 1) * DH)
        q, k = q_ref[rs, cs], k_ref[rs, cs]
        log_row = jnp.log(gate_ref[h, :, rs])
        log_col = column(log_row)
        beta_col = column(beta_ref[h, :, rs])
        sum_row = jnp.sum(jnp.where(ri <= ci, log_col, 0.0), axis=0, keepdims=True)
        sum_col = jnp.sum(jnp.where(lower, log_row, 0.0), axis=1, keepdims=True)
        total = jnp.sum(log_row, axis=1, keepdims=True)
        sk, sq = unit_scale(k), unit_scale(q)
        sk_row = as_row(sk)
        ratios = jnp.exp(jnp.where(lower, sum_col - sum_row, -1e30)) * sk_row
        both = dot(jnp.concatenate([k, q], axis=0), k, ((1,), (1,)))
        low = jnp.where(strict, (beta_col * sk) * ratios * both[:CHUNK], 0.0)
        mix = (sq * ratios) * both[CHUNK:]
        growth = jnp.exp(sum_col)
        terms[h, c] = dict(
            low=low,
            mix=mix.astype(bf16),
            inv=identity - jnp.where((ri // 2) == (ci // 2), low, 0.0),
            beta=beta_col,
            gk=growth * sk,
            gq=growth * sq,
            tail=jnp.exp(total - sum_col) * sk,
            last=jnp.exp(total),
        )
    size = 2
    while size < CHUNK:
        pick = ((ri // (2 * size)) == (ci // (2 * size))) & ((ri // size) != (ci // size))
        for u in units:
            t = terms[u]
            t["tmp"] = dot1(jnp.where(pick, t["low"], 0.0), t["inv"])
        for u in units:
            t = terms[u]
            t["inv"] = t["inv"] - dot1(t["inv"], t["tmp"])
        size *= 2
    states = [None] * HEADS_STEP
    for c in range(chunks):
        rs = slice(c * CHUNK, (c + 1) * CHUNK)
        for h in range(HEADS_STEP):
            cs = slice(h * DH, (h + 1) * DH)
            t = terms[h, c]
            q, k, v = q_ref[rs, cs], k_ref[rs, cs], v_ref[rs, cs].astype(f32)
            zero = jnp.zeros((CHUNK, DH), f32)
            if c == 0:
                state = jnp.concatenate([jnp.zeros((DH, DH), f32), identity], axis=1)
                ks = jnp.concatenate([zero, k.astype(f32)], axis=1)
                qs = jnp.concatenate([zero, q.astype(f32)], axis=1)
            else:
                state = states[h]
                sb = state.astype(bf16)
                kqs = dot(jnp.concatenate([k, q], axis=0), sb)
                ks, qs = kqs[:CHUNK], kqs[CHUNK:]
            resid = jnp.concatenate([v, zero], axis=1) - t["gk"] * ks
            errors = dot1(t["inv"], t["beta"] * resid)
            out = t["gq"] * qs + dot(t["mix"], errors.astype(bf16))
            out_ref[rs, cs] = out[:, :DH]
            qeff_ref[rs, cs] = out[:, DH:].astype(bf16)
            states[h] = t["last"] * state + dot(
                k, (t["tail"] * errors).astype(bf16), ((0,), (0,))
            )
    for h in range(HEADS_STEP):
        off_ref[h] = states[h][:, :DH]
        lin_ref[h] = states[h][:, DH:]


def delta_local(queries, keyvecs, values, gates, betas):
    rows, width = queries.shape
    heads = width // DH
    step = HEADS_STEP
    tall = pl.BlockSpec((rows, step * DH), lambda i: (0, i))
    thin = pl.BlockSpec((step, 1, rows), lambda i: (i, 0, 0))
    square = pl.BlockSpec((step, DH, DH), lambda i: (i, 0, 0))
    return pl.pallas_call(
        delta_kernel,
        grid=(heads // step,),
        in_specs=[tall, tall, tall, thin, thin],
        out_specs=[tall, tall, square, square],
        out_shape=[
            jax.ShapeDtypeStruct((rows, width), f32),
            jax.ShapeDtypeStruct((rows, width), bf16),
            jax.ShapeDtypeStruct((heads, DH, DH), f32),
            jax.ShapeDtypeStruct((heads, DH, DH), f32),
        ],
        name="delta_local",
    )(queries, keyvecs, values, gates.T[:, None, :], betas.T[:, None, :])


def attn_kernel(q_ref, k2_ref, k1_ref, k0_ref, v2_ref, v1_ref, v0_ref, out_ref, sq_ref):
    rows = q_ref.shape[0]
    me = lax.axis_index("ctx")
    bias2 = jnp.where(me >= 2, 0.0, -1e30).astype(f32)
    bias1 = jnp.where(me >= 1, 0.0, -1e30).astype(f32)
    scale = math.log2(math.e) / math.sqrt(DH)
    per = rows // QROWS
    keys = [(k2_ref, v2_ref, bias2), (k1_ref, v1_ref, bias1), (k0_ref, v0_ref, None)]
    ri = lax.broadcasted_iota(jnp.int32, (QROWS, QROWS), 0)
    ci = lax.broadcasted_iota(jnp.int32, (QROWS, QROWS), 1)
    tiles = WINDOW // QROWS + 1
    for b in range(per):
        q = q_ref[b * QROWS : (b + 1) * QROWS, :]
        scores = []
        for n in range(tiles):
            kr, vr, bias = keys[(b + n) // per]
            at = ((b + n) % per) * QROWS
            s = dot(q, kr[at : at + QROWS, :], ((1,), (1,))) * scale
            if bias is not None:
                s = s + bias
            if n == 0:
                s = jnp.where(ci > ri, s, -1e30)
            if n == tiles - 1:
                s = jnp.where(ci <= ri, s, -1e30)
            scores.append(s)
        top = functools.reduce(jnp.maximum, scores)
        top = jnp.max(top, axis=1, keepdims=True)
        raised = [jnp.exp2(s - top) for s in scores]
        total = jnp.sum(functools.reduce(jnp.add, raised), axis=1, keepdims=True)
        inverse = 1.0 / total
        out = None
        for n in range(tiles):
            kr, vr, bias = keys[(b + n) // per]
            at = ((b + n) % per) * QROWS
            part = dot((raised[n] * inverse).astype(bf16), vr[at : at + QROWS, :])
            out = part if out is None else out + part
        rs = slice(b * QROWS, (b + 1) * QROWS)
        out_ref[rs, :] = out

        @pl.when(pl.program_id(0) == 0)
        def _():
            sq_ref[rs, :] = out * out

        @pl.when(pl.program_id(0) > 0)
        def _():
            sq_ref[rs, :] += out * out


def attention(q, k2, k1, k0, v2, v1, v0):
    rows, width = q.shape
    tall = pl.BlockSpec((rows, DH), lambda i: (0, i))
    return pl.pallas_call(
        attn_kernel,
        grid=(width // DH,),
        in_specs=[tall] * 7,
        out_specs=[tall, pl.BlockSpec((rows, DH), lambda i: (0, 0))],
        out_shape=[
            jax.ShapeDtypeStruct((rows, width), f32),
            jax.ShapeDtypeStruct((rows, DH), f32),
        ],
        name="window_attention",
    )(q, k2, k1, k0, v2, v1, v0)


def fix_kernel(out_ref, qeff_ref, state_ref, full_ref, sq_ref):
    high, low = split(state_ref[0])
    q = qeff_ref[...]
    full = out_ref[...] + (dot(q, high) + dot(q, low))
    full_ref[...] = full

    @pl.when(pl.program_id(0) == 0)
    def _():
        sq_ref[...] = full * full

    @pl.when(pl.program_id(0) > 0)
    def _():
        sq_ref[...] += full * full


def add_incoming(out, qeff, state):
    rows, width = out.shape
    tall = pl.BlockSpec((rows, DH), lambda i: (0, i))
    return pl.pallas_call(
        fix_kernel,
        grid=(width // DH,),
        in_specs=[tall, tall, pl.BlockSpec((1, DH, DH), lambda i: (i, 0, 0))],
        out_specs=[tall, pl.BlockSpec((rows, DH), lambda i: (0, 0))],
        out_shape=[
            jax.ShapeDtypeStruct((rows, width), f32),
            jax.ShapeDtypeStruct((rows, DH), f32),
        ],
        name="add_incoming",
    )(out, qeff, state)


def bmm(left, right):
    return jnp.einsum("hij,hjk->hik", left, right, precision=lax.Precision.HIGH)


def incoming_state(linear, offset, axis):
    count = lax.axis_size(axis)
    me = lax.axis_index(axis)
    firsts = [(i, i + 1) for i in range(0, count - 1, 2)]
    first_linear = lax.ppermute(linear, axis, firsts)
    first_offset = lax.ppermute(offset, axis, firsts)
    pair_linear = bmm(linear, first_linear)
    pair_offset = bmm(linear, first_offset) + offset
    leaving = pair_offset
    entering = jnp.zeros_like(offset)
    for turn in range(count // 2 - 1):
        source = 2 * turn + 1
        to_odd = lax.ppermute(leaving, axis, [(source, source + 2)])
        to_even = lax.ppermute(leaving, axis, [(source, source + 1)])
        entering = entering + (to_odd + to_even)
        leaving = bmm(pair_linear, entering) + pair_offset
    return jnp.where(me % 2 == 1, bmm(first_linear, entering) + first_offset, entering)


def from_behind(value, axis, by):
    devices = lax.axis_size(axis)
    pairs = [(i, i + by) for i in range(devices) if 0 <= i + by < devices]
    return lax.ppermute(value, axis, pairs)


def on_device(
    attn_query,
    attn_key,
    attn_value,
    delta_query,
    delta_key,
    delta_value,
    delta_gate,
    delta_beta,
    attn_gain,
    delta_gain,
):
    width = attn_gain.shape[0] * lax.axis_size("head")
    k2 = from_behind(attn_key, "ctx", 2)
    k1 = from_behind(attn_key, "ctx", 1)
    v2 = from_behind(attn_value, "ctx", 2)
    v1 = from_behind(attn_value, "ctx", 1)
    local, qeff, linear, offset = delta_local(
        delta_query, delta_key, delta_value, delta_gate, delta_beta
    )
    entering = incoming_state(linear, offset, "ctx")
    attn_out, attn_sq = attention(attn_query, k2, k1, attn_key, v2, v1, attn_value)
    delta_out, delta_sq = add_incoming(local, qeff, entering)
    squares = jnp.stack([jnp.sum(attn_sq, axis=-1), jnp.sum(delta_sq, axis=-1)])
    scales = lax.rsqrt(lax.psum(squares, "head") / width + epsilon)
    joined = 0.5 * (
        attn_gain * attn_out * scales[0][:, None] + delta_gain * delta_out * scales[1][:, None]
    )
    return joined.astype(bf16)


def solution(mesh):
    both = P("ctx", "head")
    return jax.shard_map(
        on_device,
        mesh=mesh,
        in_specs=(both,) * 8 + (P("head"),) * 2,
        out_specs=both,
        check_vma=False,
    )
```

```python
import functools
import math

import jax
import jax.numpy as jnp
from jax import lax
from jax.experimental import pallas as pl
from jax.experimental.pallas import tpu as pltpu
from jax.sharding import PartitionSpec as P

DH = 128
WINDOW = 1024
CHUNK = 128
QROWS = 256
HALO_AHEAD = 12
RELAY_LAG = 3
HEADS_STEP = 2

epsilon = 1e-06
f32 = jnp.float32
bf16 = jnp.bfloat16


def dot(left, right, dims=((1,), (0,))):
    return lax.dot_general(left, right, (dims, ((), ())), preferred_element_type=f32)


def dot1(left, right, dims=((1,), (0,))):
    return dot(left.astype(bf16), right.astype(bf16), dims)


def split(value):
    high = value.astype(bf16)
    return high, (value - high.astype(f32)).astype(bf16)


def dot3(left, right, dims=((1,), (0,))):
    lh, ll = split(left)
    rh, rl = split(right)
    return dot(lh, rh, dims) + (dot(lh, rl, dims) + dot(ll, rh, dims))


def unit_scale(raw):
    wide = raw.astype(f32)
    mean = jnp.mean(wide * wide, axis=-1, keepdims=True)
    return lax.rsqrt(mean + epsilon) / math.sqrt(DH)


def delta_heads(first, q_ref, k_ref, v_ref, gate_ref, beta_ref, out_ref, qeff_ref, lin_ref, off_ref):
    rows = q_ref.shape[0]
    chunks = rows // CHUNK
    ri = lax.broadcasted_iota(jnp.int32, (CHUNK, CHUNK), 0)
    ci = lax.broadcasted_iota(jnp.int32, (CHUNK, CHUNK), 1)
    eye = ri == ci
    lower = ri >= ci
    strict = ri > ci
    identity = jnp.where(eye, 1.0, 0.0).astype(f32)

    def column(row):
        return jnp.sum(jnp.where(eye, row, 0.0), axis=1, keepdims=True)

    def as_row(col):
        return jnp.sum(jnp.where(eye, col, 0.0), axis=0, keepdims=True)

    units = [(h, c) for c in range(chunks) for h in range(HEADS_STEP)]
    terms = {}
    for h, c in units:
        rs = slice(c * CHUNK, (c + 1) * CHUNK)
        cs = pl.ds(pl.multiple_of((first + h) * DH, DH), DH)
        q, k = q_ref[rs, cs], k_ref[rs, cs]
        log_row = jnp.log(gate_ref[first + h, :, rs])
        log_col = column(log_row)
        beta_col = column(beta_ref[first + h, :, rs])
        sum_row = jnp.sum(jnp.where(ri <= ci, log_col, 0.0), axis=0, keepdims=True)
        sum_col = jnp.sum(jnp.where(lower, log_row, 0.0), axis=1, keepdims=True)
        total = jnp.sum(log_row, axis=1, keepdims=True)
        sk, sq = unit_scale(k), unit_scale(q)
        sk_row = as_row(sk)
        ratios = jnp.exp(jnp.where(lower, sum_col - sum_row, -1e30)) * sk_row
        both = dot(jnp.concatenate([k, q], axis=0), k, ((1,), (1,)))
        low = jnp.where(strict, (beta_col * sk) * ratios * both[:CHUNK], 0.0)
        mix = (sq * ratios) * both[CHUNK:]
        growth = jnp.exp(sum_col)
        terms[h, c] = dict(
            low=low,
            mix=mix.astype(bf16),
            inv=identity - jnp.where((ri // 2) == (ci // 2), low, 0.0),
            beta=beta_col,
            gk=growth * sk,
            gq=growth * sq,
            tail=jnp.exp(total - sum_col) * sk,
            last=jnp.exp(total),
        )
    size = 2
    while size < CHUNK:
        pick = ((ri // (2 * size)) == (ci // (2 * size))) & ((ri // size) != (ci // size))
        for u in units:
            t = terms[u]
            t["tmp"] = dot1(jnp.where(pick, t["low"], 0.0), t["inv"])
        for u in units:
            t = terms[u]
            t["inv"] = t["inv"] - dot1(t["inv"], t["tmp"])
        size *= 2
    states = [None] * HEADS_STEP
    for c in range(chunks):
        rs = slice(c * CHUNK, (c + 1) * CHUNK)
        for h in range(HEADS_STEP):
            cs = pl.ds(pl.multiple_of((first + h) * DH, DH), DH)
            t = terms[h, c]
            q, k, v = q_ref[rs, cs], k_ref[rs, cs], v_ref[rs, cs].astype(f32)
            zero = jnp.zeros((CHUNK, DH), f32)
            if c == 0:
                state = jnp.concatenate([jnp.zeros((DH, DH), f32), identity], axis=1)
                ks = jnp.concatenate([zero, k.astype(f32)], axis=1)
                qs = jnp.concatenate([zero, q.astype(f32)], axis=1)
            else:
                state = states[h]
                sb = state.astype(bf16)
                kqs = dot(jnp.concatenate([k, q], axis=0), sb)
                ks, qs = kqs[:CHUNK], kqs[CHUNK:]
            resid = jnp.concatenate([v, zero], axis=1) - t["gk"] * ks
            errors = dot1(t["inv"], t["beta"] * resid)
            out = t["gq"] * qs + dot(t["mix"], errors.astype(bf16))
            out_ref[first + h, rs] = out[:, :DH]
            qeff_ref[first + h, rs] = out[:, DH:].astype(bf16)
            states[h] = t["last"] * state + dot(
                k, (t["tail"] * errors).astype(bf16), ((0,), (0,))
            )
    for h in range(HEADS_STEP):
        off_ref[first + h] = states[h][:, :DH]
        lin_ref[first + h] = states[h][:, DH:]


def layer_kernel(
    aq_ref, ak_ref, av_ref, dq_ref, dk_ref, dv_ref, gate_ref, beta_ref, again_ref, dgain_ref,
    mixed_ref,
    keys, vals, attn_out, delta_out, qeff, linear, offset, entering, leaving, attn_sq, delta_sq,
    sums_send, sums_recv,
    own_sem, far_send, far_recv, near_send, near_recv, relay_send, relay_recv, sums_ss, sums_rs,
    *, contexts, groups,
):
    rows, width = aq_ref.shape
    heads = width // DH
    me = lax.axis_index("ctx")
    group = lax.axis_index("head")
    odd = lax.rem(me, 2) == 1
    even = lax.rem(me, 2) == 0
    back = WINDOW
    halves = rows // QROWS
    blocks = rows // CHUNK

    barrier = pltpu.get_barrier_semaphore()
    for by in (-2, -1, 1, 2):
        @pl.when((me + by >= 0) & (me + by < contexts))
        def _():
            pl.semaphore_signal(
                barrier, inc=1, device_id={"ctx": me + by}, device_id_type=pl.DeviceIdType.MESH
            )
    for by in range(1, groups):
        pl.semaphore_signal(
            barrier, inc=1, device_id={"head": lax.rem(group + by, groups)},
            device_id_type=pl.DeviceIdType.MESH,
        )
    near_peers = jnp.minimum(me, 2) + jnp.minimum(contexts - 1 - me, 2)
    pl.semaphore_wait(barrier, near_peers + (groups - 1))

    both = ((0, ak_ref, keys), (1, av_ref, vals))
    far_rows = pl.ds(0, rows)
    near_rows = pl.ds(rows, rows)
    own_rows = pl.ds(back, rows)

    def lanes(h):
        return pl.ds(pl.multiple_of(h * DH, DH), DH)

    def own_copy(h, kind, source, buffer):
        return pltpu.make_async_copy(
            source.at[:, lanes(h)], buffer.at[h, own_rows], own_sem.at[kind, h]
        )

    def far_copy(h, kind, source, buffer):
        return pltpu.make_async_remote_copy(
            src_ref=source.at[:, lanes(h)],
            dst_ref=buffer.at[h, far_rows],
            send_sem=far_send.at[kind, h],
            recv_sem=far_recv.at[kind, h],
            device_id={"ctx": lax.rem(me + 2, contexts)},
            device_id_type=pl.DeviceIdType.MESH,
        )

    def near_copy(h, kind, source, buffer):
        return pltpu.make_async_remote_copy(
            src_ref=source.at[:, lanes(h)],
            dst_ref=buffer.at[h, near_rows],
            send_sem=near_send.at[kind, h],
            recv_sem=near_recv.at[kind, h],
            device_id={"ctx": lax.rem(me + 1, contexts)},
            device_id_type=pl.DeviceIdType.MESH,
        )

    def forward_copy(h, kind, source, buffer):
        return pltpu.make_async_remote_copy(
            src_ref=buffer.at[h, far_rows],
            dst_ref=buffer.at[h, near_rows],
            send_sem=near_send.at[kind, h],
            recv_sem=near_recv.at[kind, h],
            device_id={"ctx": lax.rem(me + contexts - 1, contexts)},
            device_id_type=pl.DeviceIdType.MESH,
        )

    def relay_copy(h):
        return pltpu.make_async_remote_copy(
            src_ref=leaving.at[h],
            dst_ref=entering.at[h],
            send_sem=relay_send.at[h],
            recv_sem=relay_recv.at[h],
            device_id={"ctx": lax.rem(me + 1, contexts)},
            device_id_type=pl.DeviceIdType.MESH,
        )

    def send_halo(h):
        @pl.when(h < heads)
        def _():
            @pl.when(me + 2 < contexts)
            def _():
                for args in both:
                    far_copy(h, *args).start()

            @pl.when(even)
            def _():
                for args in both:
                    near_copy(h, *args).start()

    def forward(h):
        @pl.when(odd & (me >= 3))
        def _():
            for args in both:
                far_copy(h, *args).wait_recv()
                forward_copy(h, *args).start()

    def start_own(h, carry):
        for args in both:
            own_copy(h, *args).start()
        return carry

    lax.fori_loop(0, min(HALO_AHEAD, heads), lambda h, c: (send_halo(h), c)[1], 0)
    lax.fori_loop(0, heads, start_own, 0)

    @pl.when(me < 2)
    def _():
        def clear(h, carry):
            keys[h, far_rows] = jnp.zeros((rows, DH), bf16)
            vals[h, far_rows] = jnp.zeros((rows, DH), bf16)
            return carry
        lax.fori_loop(0, heads, clear, 0)

    @pl.when(me < 1)
    def _():
        def clear(h, carry):
            keys[h, near_rows] = jnp.zeros((rows, DH), bf16)
            vals[h, near_rows] = jnp.zeros((rows, DH), bf16)
            entering[h] = jnp.zeros((DH, DH), f32)
            return carry
        lax.fori_loop(0, heads, clear, 0)

    attn_sq[...] = jnp.zeros_like(attn_sq)
    delta_sq[...] = jnp.zeros_like(delta_sq)
    steps = heads // HEADS_STEP

    def delta_step(i, carry):
        delta_heads(
            i * HEADS_STEP, dq_ref, dk_ref, dv_ref, gate_ref, beta_ref,
            delta_out, qeff, linear, offset,
        )

        @pl.when(i >= 1)
        def _():
            forward(i - 1)

        send_halo(HALO_AHEAD + i)
        return carry

    lax.fori_loop(0, steps, delta_step, 0)

    scale = math.log2(math.e) / math.sqrt(DH)
    ri = lax.broadcasted_iota(jnp.int32, (QROWS, QROWS), 0)
    ci = lax.broadcasted_iota(jnp.int32, (QROWS, QROWS), 1)
    tiles = WINDOW // QROWS + 1
    first_tile = jnp.maximum(WINDOW - me * rows, 0) // QROWS

    def attend(h, b):
        q_rows = pl.ds(pl.multiple_of(b * QROWS, QROWS), QROWS)
        q = aq_ref[q_rows, lanes(h)]
        scores = []
        for n in range(tiles):
            at = pl.ds(pl.multiple_of((b + n) * QROWS, QROWS), QROWS)
            s = dot(q, keys[h, at], ((1,), (1,))) * scale
            if n < tiles - 1:
                s = s + jnp.where(b + n >= first_tile, 0.0, -1e30).astype(f32)
            if n == 0:
                s = jnp.where(ci > ri, s, -1e30)
            if n == tiles - 1:
                s = jnp.where(ci <= ri, s, -1e30)
            scores.append(s)
        top = jnp.max(functools.reduce(jnp.maximum, scores), axis=1, keepdims=True)
        raised = [jnp.exp2(s - top) for s in scores]
        total = jnp.sum(functools.reduce(jnp.add, raised), axis=1, keepdims=True)
        inverse = 1.0 / total
        out = None
        for n in range(tiles):
            at = pl.ds(pl.multiple_of((b + n) * QROWS, QROWS), QROWS)
            part = dot((raised[n] * inverse).astype(bf16), vals[h, at])
            out = part if out is None else out + part
        attn_out[h, q_rows] = out
        attn_sq[q_rows, :] += out * out

    def relay(h):
        @pl.when(me >= 1)
        def _():
            relay_copy(h).wait_recv()

        state = entering[h]

        @pl.when(me + 1 < contexts)
        def _():
            leaving[h] = dot3(linear[h], state) + offset[h]
            relay_copy(h).start()

        high, low = split(state)
        q = qeff[h]
        full = delta_out[h] + (dot(q, high) + dot(q, low))
        delta_out[h] = full
        delta_sq[...] += full * full

    def step(j, carry):
        h, b = j // halves, lax.rem(j, halves)

        @pl.when(h < heads)
        def _():
            @pl.when(b == 0)
            def _():
                @pl.when(h >= steps - 1)
                def _():
                    forward(h)

                for args in both:
                    own_copy(h, *args).wait()

                    @pl.when((me >= 2) & jnp.logical_not(odd & (me >= 3)))
                    def _():
                        far_copy(h, *args).wait_recv()

                    @pl.when(me >= 1)
                    def _():
                        near_copy(h, *args).wait_recv()

                send_halo(h + HALO_AHEAD + steps)

            attend(h, b)

        r = j - RELAY_LAG * me

        @pl.when((r >= 0) & (r < heads))
        def _():
            relay(r)

        return carry

    turns = max(heads * halves, RELAY_LAG * (contexts - 1) + heads)
    lax.fori_loop(0, turns, step, 0)

    dr = lax.broadcasted_iota(jnp.int32, (CHUNK, CHUNK), 0)
    dc = lax.broadcasted_iota(jnp.int32, (CHUNK, CHUNK), 1)
    eye = dr == dc
    lines = []
    for part in (attn_sq, delta_sq):
        for b in range(blocks):
            col = jnp.sum(part[b * CHUNK : (b + 1) * CHUNK, :], axis=1, keepdims=True)
            lines.append(jnp.sum(jnp.where(eye, col, 0.0), axis=0, keepdims=True))
    mine = jnp.concatenate(lines, axis=0)
    sums_send[...] = mine

    def sums_copy(by):
        return pltpu.make_async_remote_copy(
            src_ref=sums_send,
            dst_ref=sums_recv.at[by],
            send_sem=sums_ss.at[by],
            recv_sem=sums_rs.at[by],
            device_id={"head": lax.rem(group + by, groups)},
            device_id_type=pl.DeviceIdType.MESH,
        )

    for by in range(1, groups):
        sums_copy(by).start()
    whole = mine
    for by in range(1, groups):
        sums_copy(by).wait_recv()
        whole = whole + sums_recv[by]
    scales = lax.rsqrt(whole / (width * groups) + epsilon) * 0.5
    for b in range(blocks):
        rs = slice(b * CHUNK, (b + 1) * CHUNK)
        sa = jnp.sum(jnp.where(eye, scales[b : b + 1], 0.0), axis=1, keepdims=True)
        sd = jnp.sum(
            jnp.where(eye, scales[blocks + b : blocks + b + 1], 0.0), axis=1, keepdims=True
        )
        for h in range(heads):
            cs = slice(h * DH, (h + 1) * DH)
            mixed_ref[rs, cs] = (
                again_ref[:, cs] * attn_out[h, rs] * sa + dgain_ref[:, cs] * delta_out[h, rs] * sd
            ).astype(bf16)

    for by in range(1, groups):
        sums_copy(by).wait_send()

    def drain(h, carry):
        for args in both:
            @pl.when(me + 2 < contexts)
            def _():
                far_copy(h, *args).wait_send()

            @pl.when(even)
            def _():
                near_copy(h, *args).wait_send()

            @pl.when(odd & (me >= 3))
            def _():
                forward_copy(h, *args).wait_send()

        @pl.when(me + 1 < contexts)
        def _():
            relay_copy(h).wait_send()

        return carry

    lax.fori_loop(0, heads, drain, 0)


def on_device(
    attn_query,
    attn_key,
    attn_value,
    delta_query,
    delta_key,
    delta_value,
    delta_gate,
    delta_beta,
    attn_gain,
    delta_gain,
):
    rows, width = attn_query.shape
    heads = width // DH
    groups = lax.axis_size("head")
    lines = 2 * rows // CHUNK
    vmem = pl.BlockSpec(memory_space=pltpu.VMEM)
    hbm = pl.BlockSpec(memory_space=pl.ANY)
    dma = pltpu.SemaphoreType.DMA
    return pl.pallas_call(
        functools.partial(layer_kernel, contexts=lax.axis_size("ctx"), groups=groups),
        in_specs=[vmem, hbm, hbm] + [vmem] * 7,
        out_specs=vmem,
        out_shape=jax.ShapeDtypeStruct((rows, width), bf16),
        scratch_shapes=[
            pltpu.VMEM((heads, WINDOW + rows, DH), bf16),
            pltpu.VMEM((heads, WINDOW + rows, DH), bf16),
            pltpu.VMEM((heads, rows, DH), f32),
            pltpu.VMEM((heads, rows, DH), f32),
            pltpu.VMEM((heads, rows, DH), bf16),
            pltpu.VMEM((heads, DH, DH), f32),
            pltpu.VMEM((heads, DH, DH), f32),
            pltpu.VMEM((heads, DH, DH), f32),
            pltpu.VMEM((heads, DH, DH), f32),
            pltpu.VMEM((rows, DH), f32),
            pltpu.VMEM((rows, DH), f32),
            pltpu.VMEM((lines, CHUNK), f32),
            pltpu.VMEM((groups, lines, CHUNK), f32),
            dma((2, heads)),
            dma((2, heads)),
            dma((2, heads)),
            dma((2, heads)),
            dma((2, heads)),
            dma((heads,)),
            dma((heads,)),
            dma((groups,)),
            dma((groups,)),
        ],
        compiler_params=pltpu.CompilerParams(
            collective_id=0, has_side_effects=True, vmem_limit_bytes=60 * 1024 * 1024
        ),
        name="layer",
    )(
        attn_query,
        attn_key,
        attn_value,
        delta_query,
        delta_key,
        delta_value,
        delta_gate.T[:, None, :],
        delta_beta.T[:, None, :],
        attn_gain[None, :],
        delta_gain[None, :],
    )


def solution(mesh):
    both = P("ctx", "head")
    return jax.shard_map(
        on_device,
        mesh=mesh,
        in_specs=(both,) * 8 + (P("head"),) * 2,
        out_specs=both,
        check_vma=False,
    )
```

```python
import functools
import math

import jax
import jax.numpy as jnp
from jax import lax
from jax.experimental import pallas as pl
from jax.experimental.pallas import tpu as pltpu
from jax.sharding import PartitionSpec as P

DH = 128
WINDOW = 1024
CHUNK = 128
QROWS = 256
HALO_AHEAD = 1
RELAY_LAG = 5
HEADS_STEP = 2

epsilon = 1e-06
f32 = jnp.float32
bf16 = jnp.bfloat16


def dot(left, right, dims=((1,), (0,))):
    return lax.dot_general(left, right, (dims, ((), ())), preferred_element_type=f32)


def dot1(left, right, dims=((1,), (0,))):
    return dot(left.astype(bf16), right.astype(bf16), dims)


def split(value):
    high = value.astype(bf16)
    return high, (value - high.astype(f32)).astype(bf16)


def dot3(left, right, dims=((1,), (0,))):
    lh, ll = split(left)
    rh, rl = split(right)
    return dot(lh, rh, dims) + (dot(lh, rl, dims) + dot(ll, rh, dims))


def unit_scale(raw):
    wide = raw.astype(f32)
    mean = jnp.mean(wide * wide, axis=-1, keepdims=True)
    return lax.rsqrt(mean + epsilon) / math.sqrt(DH)


def delta_heads(first, q_ref, k_ref, v_ref, gate_ref, beta_ref, out_ref, qeff_ref, lin_ref, off_ref):
    rows = q_ref.shape[0]
    chunks = rows // CHUNK
    ri = lax.broadcasted_iota(jnp.int32, (CHUNK, CHUNK), 0)
    ci = lax.broadcasted_iota(jnp.int32, (CHUNK, CHUNK), 1)
    eye = ri == ci
    lower = ri >= ci
    strict = ri > ci
    identity = jnp.where(eye, 1.0, 0.0).astype(f32)

    def column(row):
        return jnp.sum(jnp.where(eye, row, 0.0), axis=1, keepdims=True)

    def as_row(col):
        return jnp.sum(jnp.where(eye, col, 0.0), axis=0, keepdims=True)

    units = [(h, c) for c in range(chunks) for h in range(HEADS_STEP)]
    terms = {}
    for h, c in units:
        rs = slice(c * CHUNK, (c + 1) * CHUNK)
        cs = pl.ds(pl.multiple_of((first + h) * DH, DH), DH)
        q, k = q_ref[rs, cs], k_ref[rs, cs]
        log_row = jnp.log(gate_ref[first + h, :, rs])
        log_col = column(log_row)
        beta_col = column(beta_ref[first + h, :, rs])
        sum_row = jnp.sum(jnp.where(ri <= ci, log_col, 0.0), axis=0, keepdims=True)
        sum_col = jnp.sum(jnp.where(lower, log_row, 0.0), axis=1, keepdims=True)
        total = jnp.sum(log_row, axis=1, keepdims=True)
        sk, sq = unit_scale(k), unit_scale(q)
        sk_row = as_row(sk)
        ratios = jnp.exp(jnp.where(lower, sum_col - sum_row, -1e30)) * sk_row
        both = dot(jnp.concatenate([k, q], axis=0), k, ((1,), (1,)))
        low = jnp.where(strict, (beta_col * sk) * ratios * both[:CHUNK], 0.0)
        mix = (sq * ratios) * both[CHUNK:]
        growth = jnp.exp(sum_col)
        terms[h, c] = dict(
            low=low,
            mix=mix.astype(bf16),
            inv=identity - jnp.where((ri // 2) == (ci // 2), low, 0.0),
            beta=beta_col,
            gk=growth * sk,
            gq=growth * sq,
            tail=jnp.exp(total - sum_col) * sk,
            last=jnp.exp(total),
        )
    size = 2
    while size < CHUNK:
        pick = ((ri // (2 * size)) == (ci // (2 * size))) & ((ri // size) != (ci // size))
        for u in units:
            t = terms[u]
            t["tmp"] = dot1(jnp.where(pick, t["low"], 0.0), t["inv"])
        for u in units:
            t = terms[u]
            t["inv"] = t["inv"] - dot1(t["inv"], t["tmp"])
        size *= 2
    states = [None] * HEADS_STEP
    for c in range(chunks):
        rs = slice(c * CHUNK, (c + 1) * CHUNK)
        for h in range(HEADS_STEP):
            cs = pl.ds(pl.multiple_of((first + h) * DH, DH), DH)
            t = terms[h, c]
            q, k, v = q_ref[rs, cs], k_ref[rs, cs], v_ref[rs, cs].astype(f32)
            zero = jnp.zeros((CHUNK, DH), f32)
            if c == 0:
                state = jnp.concatenate([jnp.zeros((DH, DH), f32), identity], axis=1)
                ks = jnp.concatenate([zero, k.astype(f32)], axis=1)
                qs = jnp.concatenate([zero, q.astype(f32)], axis=1)
            else:
                state = states[h]
                sb = state.astype(bf16)
                kqs = dot(jnp.concatenate([k, q], axis=0), sb)
                ks, qs = kqs[:CHUNK], kqs[CHUNK:]
            resid = jnp.concatenate([v, zero], axis=1) - t["gk"] * ks
            errors = dot1(t["inv"], t["beta"] * resid)
            out = t["gq"] * qs + dot(t["mix"], errors.astype(bf16))
            out_ref[first + h, rs] = out[:, :DH]
            qeff_ref[first + h, rs] = out[:, DH:].astype(bf16)
            states[h] = t["last"] * state + dot(
                k, (t["tail"] * errors).astype(bf16), ((0,), (0,))
            )
    for h in range(HEADS_STEP):
        off_ref[first + h] = states[h][:, :DH]
        lin_ref[first + h] = states[h][:, DH:]


def layer_kernel(
    aq_ref, ak_ref, av_ref, dq_ref, dk_ref, dv_ref, gates_ref, betas_ref, again_ref, dgain_ref,
    mixed_hbm,
    keys, vals, attn_out, delta_out, qeff, linear, offset, entering, leaving, attn_sq, delta_sq,
    sums_send, sums_recv, gate_ref, beta_ref, mixed_ref,
    out_sem, own_sem, far_send, far_recv, near_send, near_recv, relay_send, relay_recv, sums_ss, sums_rs,
    *, contexts, groups,
):
    rows, width = aq_ref.shape
    heads = width // DH
    me = lax.axis_index("ctx")
    group = lax.axis_index("head")
    odd = lax.rem(me, 2) == 1
    even = lax.rem(me, 2) == 0
    back = WINDOW
    halves = rows // QROWS
    blocks = rows // CHUNK

    both = ((0, ak_ref, keys), (1, av_ref, vals))
    far_rows = pl.ds(0, rows)
    near_rows = pl.ds(rows, rows)
    own_rows = pl.ds(back, rows)

    def lanes(h):
        return pl.ds(pl.multiple_of(h * DH, DH), DH)

    def own_copy(h, kind, source, buffer):
        return pltpu.make_async_copy(
            source.at[:, lanes(h)], buffer.at[h, own_rows], own_sem.at[kind, h]
        )

    def far_copy(h, kind, source, buffer):
        return pltpu.make_async_remote_copy(
            src_ref=buffer.at[h, own_rows],
            dst_ref=buffer.at[h, far_rows],
            send_sem=far_send.at[kind, h],
            recv_sem=far_recv.at[kind, h],
            device_id={"ctx": lax.rem(me + 2, contexts)},
            device_id_type=pl.DeviceIdType.MESH,
        )

    def near_copy(h, kind, source, buffer):
        return pltpu.make_async_remote_copy(
            src_ref=buffer.at[h, own_rows],
            dst_ref=buffer.at[h, near_rows],
            send_sem=near_send.at[kind, h],
            recv_sem=near_recv.at[kind, h],
            device_id={"ctx": lax.rem(me + 1, contexts)},
            device_id_type=pl.DeviceIdType.MESH,
        )

    def forward_copy(h, kind, source, buffer):
        return pltpu.make_async_remote_copy(
            src_ref=buffer.at[h, far_rows],
            dst_ref=buffer.at[h, near_rows],
            send_sem=near_send.at[kind, h],
            recv_sem=near_recv.at[kind, h],
            device_id={"ctx": lax.rem(me + contexts - 1, contexts)},
            device_id_type=pl.DeviceIdType.MESH,
        )

    def relay_copy(h):
        return pltpu.make_async_remote_copy(
            src_ref=leaving.at[h],
            dst_ref=entering.at[h],
            send_sem=relay_send.at[h],
            recv_sem=relay_recv.at[h],
            device_id={"ctx": lax.rem(me + 1, contexts)},
            device_id_type=pl.DeviceIdType.MESH,
        )

    def send_halo(h):
        @pl.when(h < heads)
        def _():
            @pl.when(me + 2 < contexts)
            def _():
                for args in both:
                    far_copy(h, *args).start()

            @pl.when(even)
            def _():
                for args in both:
                    near_copy(h, *args).start()

    def forward(h):
        @pl.when(odd & (me >= 3))
        def _():
            for args in both:
                far_copy(h, *args).wait_recv()
                forward_copy(h, *args).start()

    def start_own(h, carry):
        for args in both:
            own_copy(h, *args).start()
        return carry

    lax.fori_loop(0, heads, start_own, 0)

    barrier = pltpu.get_barrier_semaphore()
    for by in (-2, -1, 1, 2):
        @pl.when((me + by >= 0) & (me + by < contexts))
        def _():
            pl.semaphore_signal(
                barrier, inc=1, device_id={"ctx": me + by}, device_id_type=pl.DeviceIdType.MESH
            )
    for by in range(1, groups):
        pl.semaphore_signal(
            barrier, inc=1, device_id={"head": lax.rem(group + by, groups)},
            device_id_type=pl.DeviceIdType.MESH,
        )
    near_peers = jnp.minimum(me, 2) + jnp.minimum(contexts - 1 - me, 2)
    pl.semaphore_wait(barrier, near_peers + (groups - 1))

    def wait_own(h, carry):
        for args in both:
            own_copy(h, *args).wait()
        return carry

    lax.fori_loop(0, heads, wait_own, 0)
    lax.fori_loop(0, min(HALO_AHEAD, heads), lambda h, c: (send_halo(h), c)[1], 0)

    @pl.when(me < 2)
    def _():
        def clear(h, carry):
            keys[h, far_rows] = jnp.zeros((rows, DH), bf16)
            vals[h, far_rows] = jnp.zeros((rows, DH), bf16)
            return carry
        lax.fori_loop(0, heads, clear, 0)

    @pl.when(me < 1)
    def _():
        def clear(h, carry):
            keys[h, near_rows] = jnp.zeros((rows, DH), bf16)
            vals[h, near_rows] = jnp.zeros((rows, DH), bf16)
            entering[h] = jnp.zeros((DH, DH), f32)
            return carry
        lax.fori_loop(0, heads, clear, 0)

    gate_rows, beta_rows = gates_ref[...].T, betas_ref[...].T
    for h in range(heads):
        gate_ref[h] = gate_rows[h : h + 1]
        beta_ref[h] = beta_rows[h : h + 1]
    attn_sq[...] = jnp.zeros_like(attn_sq)
    delta_sq[...] = jnp.zeros_like(delta_sq)
    steps = heads // HEADS_STEP

    def delta_step(i, carry):
        delta_heads(
            i * HEADS_STEP, dq_ref, dk_ref, dv_ref, gate_ref, beta_ref,
            delta_out, qeff, linear, offset,
        )

        @pl.when(i >= 1)
        def _():
            forward(i - 1)

        send_halo(HALO_AHEAD + i)
        return carry

    lax.fori_loop(0, steps, delta_step, 0)

    scale = math.log2(math.e) / math.sqrt(DH)
    ri = lax.broadcasted_iota(jnp.int32, (QROWS, QROWS), 0)
    ci = lax.broadcasted_iota(jnp.int32, (QROWS, QROWS), 1)
    tiles = WINDOW // QROWS + 1
    first_tile = jnp.maximum(WINDOW - me * rows, 0) // QROWS

    def attend(h, b):
        q_rows = pl.ds(pl.multiple_of(b * QROWS, QROWS), QROWS)
        q = aq_ref[q_rows, lanes(h)]
        scores = []
        for n in range(tiles):
            at = pl.ds(pl.multiple_of((b + n) * QROWS, QROWS), QROWS)
            s = dot(q, keys[h, at], ((1,), (1,))) * scale
            if n < tiles - 1:
                s = s + jnp.where(b + n >= first_tile, 0.0, -1e30).astype(f32)
            if n == 0:
                s = jnp.where(ci > ri, s, -1e30)
            if n == tiles - 1:
                s = jnp.where(ci <= ri, s, -1e30)
            scores.append(s)
        top = jnp.max(functools.reduce(jnp.maximum, scores), axis=1, keepdims=True)
        raised = [jnp.exp2(s - top) for s in scores]
        total = jnp.sum(functools.reduce(jnp.add, raised), axis=1, keepdims=True)
        inverse = 1.0 / total
        out = None
        for n in range(tiles):
            at = pl.ds(pl.multiple_of((b + n) * QROWS, QROWS), QROWS)
            part = dot((raised[n] * inverse).astype(bf16), vals[h, at])
            out = part if out is None else out + part
        attn_out[h, q_rows] = out
        attn_sq[q_rows, :] += out * out

    def relay(h):
        @pl.when(me >= 1)
        def _():
            relay_copy(h).wait_recv()

        state = entering[h]

        @pl.when(me + 1 < contexts)
        def _():
            leaving[h] = dot3(linear[h], state) + offset[h]
            relay_copy(h).start()

        high, low = split(state)
        q = qeff[h]
        full = delta_out[h] + (dot(q, high) + dot(q, low))
        delta_out[h] = full
        delta_sq[...] += full * full

    def step(j, carry):
        h, b = j // halves, lax.rem(j, halves)

        @pl.when(h < heads)
        def _():
            @pl.when(b == 0)
            def _():
                @pl.when(h >= steps - 1)
                def _():
                    forward(h)

                for args in both:
                    @pl.when((me >= 2) & jnp.logical_not(odd & (me >= 3)))
                    def _():
                        far_copy(h, *args).wait_recv()

                    @pl.when(me >= 1)
                    def _():
                        near_copy(h, *args).wait_recv()

                send_halo(h + HALO_AHEAD + steps)

            attend(h, b)

        r = j - RELAY_LAG * me

        @pl.when((r >= 0) & (r < heads))
        def _():
            relay(r)

        return carry

    turns = max(heads * halves, RELAY_LAG * (contexts - 1) + heads)
    lax.fori_loop(0, turns, step, 0)

    dr = lax.broadcasted_iota(jnp.int32, (CHUNK, CHUNK), 0)
    dc = lax.broadcasted_iota(jnp.int32, (CHUNK, CHUNK), 1)
    eye = dr == dc
    lines = []
    for part in (attn_sq, delta_sq):
        for b in range(blocks):
            col = jnp.sum(part[b * CHUNK : (b + 1) * CHUNK, :], axis=1, keepdims=True)
            lines.append(jnp.sum(jnp.where(eye, col, 0.0), axis=0, keepdims=True))
    mine = jnp.concatenate(lines, axis=0)
    sums_send[...] = mine

    def sums_copy(by):
        return pltpu.make_async_remote_copy(
            src_ref=sums_send,
            dst_ref=sums_recv.at[by],
            send_sem=sums_ss.at[by],
            recv_sem=sums_rs.at[by],
            device_id={"head": lax.rem(group + by, groups)},
            device_id_type=pl.DeviceIdType.MESH,
        )

    for by in range(1, groups):
        sums_copy(by).start()
    whole = mine
    for by in range(1, groups):
        sums_copy(by).wait_recv()
        whole = whole + sums_recv[by]
    scales = lax.rsqrt(whole / (width * groups) + epsilon) * 0.5

    def out_copy(b):
        span = pl.ds(b * CHUNK, CHUNK)
        return pltpu.make_async_copy(mixed_ref.at[span], mixed_hbm.at[span], out_sem.at[b])

    for b in range(blocks):
        rs = slice(b * CHUNK, (b + 1) * CHUNK)
        sa = jnp.sum(jnp.where(eye, scales[b : b + 1], 0.0), axis=1, keepdims=True)
        sd = jnp.sum(
            jnp.where(eye, scales[blocks + b : blocks + b + 1], 0.0), axis=1, keepdims=True
        )
        for h in range(heads):
            cs = slice(h * DH, (h + 1) * DH)
            mixed_ref[rs, cs] = (
                again_ref[cs][None, :] * attn_out[h, rs] * sa + dgain_ref[cs][None, :] * delta_out[h, rs] * sd
            ).astype(bf16)
        out_copy(b).start()

    for b in range(blocks):
        out_copy(b).wait()
    for by in range(1, groups):
        sums_copy(by).wait_send()

    def drain(h, carry):
        for args in both:
            @pl.when(me + 2 < contexts)
            def _():
                far_copy(h, *args).wait_send()

            @pl.when(even)
            def _():
                near_copy(h, *args).wait_send()

            @pl.when(odd & (me >= 3))
            def _():
                forward_copy(h, *args).wait_send()

        @pl.when(me + 1 < contexts)
        def _():
            relay_copy(h).wait_send()

        return carry

    lax.fori_loop(0, heads, drain, 0)


def on_device(
    attn_query,
    attn_key,
    attn_value,
    delta_query,
    delta_key,
    delta_value,
    delta_gate,
    delta_beta,
    attn_gain,
    delta_gain,
):
    rows, width = attn_query.shape
    heads = width // DH
    groups = lax.axis_size("head")
    lines = 2 * rows // CHUNK
    vmem = pl.BlockSpec(memory_space=pltpu.VMEM)
    hbm = pl.BlockSpec(memory_space=pl.ANY)
    dma = pltpu.SemaphoreType.DMA
    return pl.pallas_call(
        functools.partial(layer_kernel, contexts=lax.axis_size("ctx"), groups=groups),
        in_specs=[vmem, hbm, hbm] + [vmem] * 7,
        out_specs=hbm,
        out_shape=jax.ShapeDtypeStruct((rows, width), bf16),
        scratch_shapes=[
            pltpu.VMEM((heads, WINDOW + rows, DH), bf16),
            pltpu.VMEM((heads, WINDOW + rows, DH), bf16),
            pltpu.VMEM((heads, rows, DH), f32),
            pltpu.VMEM((heads, rows, DH), f32),
            pltpu.VMEM((heads, rows, DH), bf16),
            pltpu.VMEM((heads, DH, DH), f32),
            pltpu.VMEM((heads, DH, DH), f32),
            pltpu.VMEM((heads, DH, DH), f32),
            pltpu.VMEM((heads, DH, DH), f32),
            pltpu.VMEM((rows, DH), f32),
            pltpu.VMEM((rows, DH), f32),
            pltpu.VMEM((lines, CHUNK), f32),
            pltpu.VMEM((groups, lines, CHUNK), f32),
            pltpu.VMEM((heads, 1, rows), f32),
            pltpu.VMEM((heads, 1, rows), f32),
            pltpu.VMEM((rows, width), bf16),
            dma((rows // CHUNK,)),
            dma((2, heads)),
            dma((2, heads)),
            dma((2, heads)),
            dma((2, heads)),
            dma((2, heads)),
            dma((heads,)),
            dma((heads,)),
            dma((groups,)),
            dma((groups,)),
        ],
        compiler_params=pltpu.CompilerParams(
            collective_id=0, has_side_effects=True, vmem_limit_bytes=60 * 1024 * 1024
        ),
        name="layer",
    )(
        attn_query,
        attn_key,
        attn_value,
        delta_query,
        delta_key,
        delta_value,
        delta_gate,
        delta_beta,
        attn_gain,
        delta_gain,
    )


def solution(mesh):
    both = P("ctx", "head")
    return jax.shard_map(
        on_device,
        mesh=mesh,
        in_specs=(both,) * 8 + (P("head"),) * 2,
        out_specs=both,
        check_vma=False,
    )
```

```python
import functools
import math

import jax
import jax.numpy as jnp
from jax import lax
from jax.experimental import pallas as pl
from jax.experimental.pallas import tpu as pltpu
from jax.sharding import PartitionSpec as P

DH = 128
WINDOW = 1024
CHUNK = 128
QROWS = 256
HALO_AHEAD = 2
RELAY_LAG = 5
HEADS_STEP = 2

epsilon = 1e-06
f32 = jnp.float32
bf16 = jnp.bfloat16


def dot(left, right, dims=((1,), (0,))):
    return lax.dot_general(left, right, (dims, ((), ())), preferred_element_type=f32)


def dot1(left, right, dims=((1,), (0,))):
    return dot(left.astype(bf16), right.astype(bf16), dims)


def split(value):
    high = value.astype(bf16)
    return high, (value - high.astype(f32)).astype(bf16)


def dot3(left, right, dims=((1,), (0,))):
    lh, ll = split(left)
    rh, rl = split(right)
    return dot(lh, rh, dims) + (dot(lh, rl, dims) + dot(ll, rh, dims))


def unit_scale(raw):
    wide = raw.astype(f32)
    mean = jnp.mean(wide * wide, axis=-1, keepdims=True)
    return lax.rsqrt(mean + epsilon) / math.sqrt(DH)


def delta_heads(first, q_ref, k_ref, v_ref, gate_ref, beta_ref, out_ref, qeff_ref, lin_ref, off_ref):
    rows = q_ref.shape[0]
    chunks = rows // CHUNK
    ri = lax.broadcasted_iota(jnp.int32, (CHUNK, CHUNK), 0)
    ci = lax.broadcasted_iota(jnp.int32, (CHUNK, CHUNK), 1)
    eye = ri == ci
    lower = ri >= ci
    strict = ri > ci
    identity = jnp.where(eye, 1.0, 0.0).astype(f32)

    def column(row):
        return jnp.sum(jnp.where(eye, row, 0.0), axis=1, keepdims=True)

    def as_row(col):
        return jnp.sum(jnp.where(eye, col, 0.0), axis=0, keepdims=True)

    units = [(h, c) for c in range(chunks) for h in range(HEADS_STEP)]
    terms = {}
    for h, c in units:
        rs = slice(c * CHUNK, (c + 1) * CHUNK)
        cs = pl.ds(pl.multiple_of((first + h) * DH, DH), DH)
        q, k = q_ref[rs, cs], k_ref[rs, cs]
        log_row = jnp.log(gate_ref[first + h, :, rs])
        log_col = column(log_row)
        beta_col = column(beta_ref[first + h, :, rs])
        sum_row = jnp.sum(jnp.where(ri <= ci, log_col, 0.0), axis=0, keepdims=True)
        sum_col = jnp.sum(jnp.where(lower, log_row, 0.0), axis=1, keepdims=True)
        total = jnp.sum(log_row, axis=1, keepdims=True)
        sk, sq = unit_scale(k), unit_scale(q)
        sk_row = as_row(sk)
        ratios = jnp.exp(jnp.where(lower, sum_col - sum_row, -1e30)) * sk_row
        both = dot(jnp.concatenate([k, q], axis=0), k, ((1,), (1,)))
        low = jnp.where(strict, (beta_col * sk) * ratios * both[:CHUNK], 0.0)
        mix = (sq * ratios) * both[CHUNK:]
        growth = jnp.exp(sum_col)
        terms[h, c] = dict(
            low=low,
            mix=mix.astype(bf16),
            inv=identity - jnp.where((ri // 2) == (ci // 2), low, 0.0),
            beta=beta_col,
            gk=growth * sk,
            gq=growth * sq,
            tail=jnp.exp(total - sum_col) * sk,
            last=jnp.exp(total),
        )
    size = 2
    while size < CHUNK:
        pick = ((ri // (2 * size)) == (ci // (2 * size))) & ((ri // size) != (ci // size))
        for u in units:
            t = terms[u]
            t["tmp"] = dot1(jnp.where(pick, t["low"], 0.0), t["inv"])
        for u in units:
            t = terms[u]
            t["inv"] = t["inv"] - dot1(t["inv"], t["tmp"])
        size *= 2
    states = [None] * HEADS_STEP
    for c in range(chunks):
        rs = slice(c * CHUNK, (c + 1) * CHUNK)
        for h in range(HEADS_STEP):
            cs = pl.ds(pl.multiple_of((first + h) * DH, DH), DH)
            t = terms[h, c]
            q, k, v = q_ref[rs, cs], k_ref[rs, cs], v_ref[rs, cs].astype(f32)
            zero = jnp.zeros((CHUNK, DH), f32)
            if c == 0:
                state = jnp.concatenate([jnp.zeros((DH, DH), f32), identity], axis=1)
                ks = jnp.concatenate([zero, k.astype(f32)], axis=1)
                qs = jnp.concatenate([zero, q.astype(f32)], axis=1)
            else:
                state = states[h]
                sb = state.astype(bf16)
                kqs = dot(jnp.concatenate([k, q], axis=0), sb)
                ks, qs = kqs[:CHUNK], kqs[CHUNK:]
            resid = jnp.concatenate([v, zero], axis=1) - t["gk"] * ks
            errors = dot1(t["inv"], t["beta"] * resid)
            out = t["gq"] * qs + dot(t["mix"], errors.astype(bf16))
            out_ref[first + h, rs] = out[:, :DH]
            qeff_ref[first + h, rs] = out[:, DH:].astype(bf16)
            states[h] = t["last"] * state + dot(
                k, (t["tail"] * errors).astype(bf16), ((0,), (0,))
            )
    for h in range(HEADS_STEP):
        off_ref[first + h] = states[h][:, :DH]
        lin_ref[first + h] = states[h][:, DH:]


def layer_kernel(
    aq_ref, ak_ref, av_ref, dq_ref, dk_ref, dv_ref, gates_ref, betas_ref, again_ref, dgain_ref,
    mixed_hbm,
    keys, vals, attn_out, delta_out, qeff, linear, offset, entering, leaving, attn_sq, delta_sq,
    sums_send, sums_recv, gate_ref, beta_ref, mixed_ref,
    out_sem, own_sem, far_send, far_recv, near_send, near_recv, relay_send, relay_recv, sums_ss, sums_rs,
    *, contexts, groups,
):
    rows, width = aq_ref.shape
    heads = width // DH
    me = lax.axis_index("ctx")
    group = lax.axis_index("head")
    odd = lax.rem(me, 2) == 1
    even = lax.rem(me, 2) == 0
    back = WINDOW
    halves = rows // QROWS
    blocks = rows // CHUNK

    both = ((0, ak_ref, keys), (1, av_ref, vals))
    far_rows = pl.ds(0, rows)
    near_rows = pl.ds(rows, rows)
    own_rows = pl.ds(back, rows)

    def lanes(h):
        return pl.ds(pl.multiple_of(h * DH, DH), DH)

    def own_copy(h, kind, source, buffer):
        return pltpu.make_async_copy(
            source.at[:, lanes(h)], buffer.at[h, own_rows], own_sem.at[kind, h]
        )

    def far_copy(h, kind, source, buffer):
        return pltpu.make_async_remote_copy(
            src_ref=buffer.at[h, own_rows],
            dst_ref=buffer.at[h, far_rows],
            send_sem=far_send.at[kind, h],
            recv_sem=far_recv.at[kind, h],
            device_id={"ctx": lax.rem(me + 2, contexts)},
            device_id_type=pl.DeviceIdType.MESH,
        )

    def near_copy(h, kind, source, buffer):
        return pltpu.make_async_remote_copy(
            src_ref=buffer.at[h, own_rows],
            dst_ref=buffer.at[h, near_rows],
            send_sem=near_send.at[kind, h],
            recv_sem=near_recv.at[kind, h],
            device_id={"ctx": lax.rem(me + 1, contexts)},
            device_id_type=pl.DeviceIdType.MESH,
        )

    def forward_copy(h, kind, source, buffer):
        return pltpu.make_async_remote_copy(
            src_ref=buffer.at[h, far_rows],
            dst_ref=buffer.at[h, near_rows],
            send_sem=near_send.at[kind, h],
            recv_sem=near_recv.at[kind, h],
            device_id={"ctx": lax.rem(me + contexts - 1, contexts)},
            device_id_type=pl.DeviceIdType.MESH,
        )

    def relay_copy(h):
        return pltpu.make_async_remote_copy(
            src_ref=leaving.at[h],
            dst_ref=entering.at[h],
            send_sem=relay_send.at[h],
            recv_sem=relay_recv.at[h],
            device_id={"ctx": lax.rem(me + 1, contexts)},
            device_id_type=pl.DeviceIdType.MESH,
        )

    def send_halo(h):
        @pl.when(h < heads)
        def _():
            @pl.when(me + 2 < contexts)
            def _():
                for args in both:
                    far_copy(h, *args).start()

            @pl.when(even)
            def _():
                for args in both:
                    near_copy(h, *args).start()

    def forward(h):
        @pl.when(odd & (me >= 3))
        def _():
            for args in both:
                far_copy(h, *args).wait_recv()
                forward_copy(h, *args).start()

    def start_own(h, carry):
        for args in both:
            own_copy(h, *args).start()
        return carry

    lax.fori_loop(0, heads, start_own, 0)

    barrier = pltpu.get_barrier_semaphore()
    for by in (-2, -1, 1, 2):
        @pl.when((me + by >= 0) & (me + by < contexts))
        def _():
            pl.semaphore_signal(
                barrier, inc=1, device_id={"ctx": me + by}, device_id_type=pl.DeviceIdType.MESH
            )
    for by in range(1, groups):
        pl.semaphore_signal(
            barrier, inc=1, device_id={"head": lax.rem(group + by, groups)},
            device_id_type=pl.DeviceIdType.MESH,
        )
    near_peers = jnp.minimum(me, 2) + jnp.minimum(contexts - 1 - me, 2)
    pl.semaphore_wait(barrier, near_peers + (groups - 1))

    def wait_own(h, carry):
        for args in both:
            own_copy(h, *args).wait()
        return carry

    lax.fori_loop(0, heads, wait_own, 0)
    lax.fori_loop(0, min(HALO_AHEAD, heads), lambda h, c: (send_halo(h), c)[1], 0)

    @pl.when(me < 2)
    def _():
        def clear(h, carry):
            keys[h, far_rows] = jnp.zeros((rows, DH), bf16)
            vals[h, far_rows] = jnp.zeros((rows, DH), bf16)
            return carry
        lax.fori_loop(0, heads, clear, 0)

    @pl.when(me < 1)
    def _():
        def clear(h, carry):
            keys[h, near_rows] = jnp.zeros((rows, DH), bf16)
            vals[h, near_rows] = jnp.zeros((rows, DH), bf16)
            entering[h] = jnp.zeros((DH, DH), f32)
            return carry
        lax.fori_loop(0, heads, clear, 0)

    gate_rows, beta_rows = gates_ref[...].T, betas_ref[...].T
    for h in range(heads):
        gate_ref[h] = gate_rows[h : h + 1]
        beta_ref[h] = beta_rows[h : h + 1]
    attn_sq[...] = jnp.zeros_like(attn_sq)
    delta_sq[...] = jnp.zeros_like(delta_sq)
    steps = heads // HEADS_STEP

    def delta_step(i, carry):
        delta_heads(
            i * HEADS_STEP, dq_ref, dk_ref, dv_ref, gate_ref, beta_ref,
            delta_out, qeff, linear, offset,
        )

        @pl.when(i >= 1)
        def _():
            forward(i - 1)

        send_halo(HALO_AHEAD + i)
        return carry

    lax.fori_loop(0, steps, delta_step, 0)

    scale = math.log2(math.e) / math.sqrt(DH)
    ri = lax.broadcasted_iota(jnp.int32, (QROWS, QROWS), 0)
    ci = lax.broadcasted_iota(jnp.int32, (QROWS, QROWS), 1)
    tiles = WINDOW // QROWS + 1
    first_tile = jnp.maximum(WINDOW - me * rows, 0) // QROWS

    def attend(h, b):
        q_rows = pl.ds(pl.multiple_of(b * QROWS, QROWS), QROWS)
        q = aq_ref[q_rows, lanes(h)]
        scores = []
        for n in range(tiles):
            at = pl.ds(pl.multiple_of((b + n) * QROWS, QROWS), QROWS)
            s = dot(q, keys[h, at], ((1,), (1,))) * scale
            if n < tiles - 1:
                s = s + jnp.where(b + n >= first_tile, 0.0, -1e30).astype(f32)
            if n == 0:
                s = jnp.where(ci > ri, s, -1e30)
            if n == tiles - 1:
                s = jnp.where(ci <= ri, s, -1e30)
            scores.append(s)
        top = jnp.max(functools.reduce(jnp.maximum, scores), axis=1, keepdims=True)
        raised = [jnp.exp2(s - top) for s in scores]
        total = jnp.sum(functools.reduce(jnp.add, raised), axis=1, keepdims=True)
        inverse = 1.0 / total
        out = None
        for n in range(tiles):
            at = pl.ds(pl.multiple_of((b + n) * QROWS, QROWS), QROWS)
            part = dot((raised[n] * inverse).astype(bf16), vals[h, at])
            out = part if out is None else out + part
        attn_out[h, q_rows] = out
        attn_sq[q_rows, :] += out * out

    def relay(h):
        @pl.when(me >= 1)
        def _():
            relay_copy(h).wait_recv()

        state = entering[h]

        @pl.when(me + 1 < contexts)
        def _():
            leaving[h] = dot3(linear[h], state) + offset[h]
            relay_copy(h).start()

        high, low = split(state)
        q = qeff[h]
        full = delta_out[h] + (dot(q, high) + dot(q, low))
        delta_out[h] = full
        delta_sq[...] += full * full

    def step(j, carry):
        h, b = j // halves, lax.rem(j, halves)

        @pl.when(h < heads)
        def _():
            @pl.when(b == 0)
            def _():
                @pl.when(h >= steps - 1)
                def _():
                    forward(h)

                for args in both:
                    @pl.when((me >= 2) & jnp.logical_not(odd & (me >= 3)))
                    def _():
                        far_copy(h, *args).wait_recv()

                    @pl.when(me >= 1)
                    def _():
                        near_copy(h, *args).wait_recv()

                send_halo(h + HALO_AHEAD + steps)

            attend(h, b)

        r = j - RELAY_LAG * me

        @pl.when((r >= 0) & (r < heads))
        def _():
            relay(r)

        return carry

    turns = max(heads * halves, RELAY_LAG * (contexts - 1) + heads)
    lax.fori_loop(0, turns, step, 0)

    dr = lax.broadcasted_iota(jnp.int32, (CHUNK, CHUNK), 0)
    dc = lax.broadcasted_iota(jnp.int32, (CHUNK, CHUNK), 1)
    eye = dr == dc
    lines = []
    for part in (attn_sq, delta_sq):
        for b in range(blocks):
            col = jnp.sum(part[b * CHUNK : (b + 1) * CHUNK, :], axis=1, keepdims=True)
            lines.append(jnp.sum(jnp.where(eye, col, 0.0), axis=0, keepdims=True))
    mine = jnp.concatenate(lines, axis=0)
    sums_send[...] = mine

    def sums_copy(by):
        return pltpu.make_async_remote_copy(
            src_ref=sums_send,
            dst_ref=sums_recv.at[by],
            send_sem=sums_ss.at[by],
            recv_sem=sums_rs.at[by],
            device_id={"head": lax.rem(group + by, groups)},
            device_id_type=pl.DeviceIdType.MESH,
        )

    for by in range(1, groups):
        sums_copy(by).start()
    whole = mine
    for by in range(1, groups):
        sums_copy(by).wait_recv()
        whole = whole + sums_recv[by]
    scales = lax.rsqrt(whole / (width * groups) + epsilon) * 0.5

    def out_copy(b):
        span = pl.ds(b * CHUNK, CHUNK)
        return pltpu.make_async_copy(mixed_ref.at[span], mixed_hbm.at[span], out_sem.at[b])

    for b in range(blocks):
        rs = slice(b * CHUNK, (b + 1) * CHUNK)
        sa = jnp.sum(jnp.where(eye, scales[b : b + 1], 0.0), axis=1, keepdims=True)
        sd = jnp.sum(
            jnp.where(eye, scales[blocks + b : blocks + b + 1], 0.0), axis=1, keepdims=True
        )
        for h in range(heads):
            cs = slice(h * DH, (h + 1) * DH)
            mixed_ref[rs, cs] = (
                again_ref[cs][None, :] * attn_out[h, rs] * sa + dgain_ref[cs][None, :] * delta_out[h, rs] * sd
            ).astype(bf16)
        out_copy(b).start()

    for b in range(blocks):
        out_copy(b).wait()
    for by in range(1, groups):
        sums_copy(by).wait_send()

    def drain(h, carry):
        for args in both:
            @pl.when(me + 2 < contexts)
            def _():
                far_copy(h, *args).wait_send()

            @pl.when(even)
            def _():
                near_copy(h, *args).wait_send()

            @pl.when(odd & (me >= 3))
            def _():
                forward_copy(h, *args).wait_send()

        @pl.when(me + 1 < contexts)
        def _():
            relay_copy(h).wait_send()

        return carry

    lax.fori_loop(0, heads, drain, 0)


def on_device(
    attn_query,
    attn_key,
    attn_value,
    delta_query,
    delta_key,
    delta_value,
    delta_gate,
    delta_beta,
    attn_gain,
    delta_gain,
):
    rows, width = attn_query.shape
    heads = width // DH
    groups = lax.axis_size("head")
    lines = 2 * rows // CHUNK
    vmem = pl.BlockSpec(memory_space=pltpu.VMEM)
    hbm = pl.BlockSpec(memory_space=pl.ANY)
    dma = pltpu.SemaphoreType.DMA
    return pl.pallas_call(
        functools.partial(layer_kernel, contexts=lax.axis_size("ctx"), groups=groups),
        in_specs=[vmem, hbm, hbm] + [vmem] * 7,
        out_specs=hbm,
        out_shape=jax.ShapeDtypeStruct((rows, width), bf16),
        scratch_shapes=[
            pltpu.VMEM((heads, WINDOW + rows, DH), bf16),
            pltpu.VMEM((heads, WINDOW + rows, DH), bf16),
            pltpu.VMEM((heads, rows, DH), f32),
            pltpu.VMEM((heads, rows, DH), f32),
            pltpu.VMEM((heads, rows, DH), bf16),
            pltpu.VMEM((heads, DH, DH), f32),
            pltpu.VMEM((heads, DH, DH), f32),
            pltpu.VMEM((heads, DH, DH), f32),
            pltpu.VMEM((heads, DH, DH), f32),
            pltpu.VMEM((rows, DH), f32),
            pltpu.VMEM((rows, DH), f32),
            pltpu.VMEM((lines, CHUNK), f32),
            pltpu.VMEM((groups, lines, CHUNK), f32),
            pltpu.VMEM((heads, 1, rows), f32),
            pltpu.VMEM((heads, 1, rows), f32),
            pltpu.VMEM((rows, width), bf16),
            dma((rows // CHUNK,)),
            dma((2, heads)),
            dma((2, heads)),
            dma((2, heads)),
            dma((2, heads)),
            dma((2, heads)),
            dma((heads,)),
            dma((heads,)),
            dma((groups,)),
            dma((groups,)),
        ],
        compiler_params=pltpu.CompilerParams(
            collective_id=0, has_side_effects=True, vmem_limit_bytes=60 * 1024 * 1024
        ),
        name="layer",
    )(
        attn_query,
        attn_key,
        attn_value,
        delta_query,
        delta_key,
        delta_value,
        delta_gate,
        delta_beta,
        attn_gain,
        delta_gain,
    )


def solution(mesh):
    both = P("ctx", "head")
    return jax.shard_map(
        on_device,
        mesh=mesh,
        in_specs=(both,) * 8 + (P("head"),) * 2,
        out_specs=both,
        check_vma=False,
    )
```
